32 devices in a mesh: ctx: 8 (over y, x, core), head: 4 (over z).
Axes of the slice: x: 2, y: 2, z: 4, core: 2. Of those that a mesh axis runs over, the one named last changes fastest.
Arguments:
- queries: bfloat16 [3072, 8192], P('ctx', 'head'), may hold values from -45 to 45
- keys: bfloat16 [3072, 1024], P('ctx', 'head'), may hold values from -4 to 4
- values: bfloat16 [3072, 1024], P('ctx', 'head'), may hold values from -16 to 16
- gate_mask: int32 [64], P('head'), may hold values 0 or 1
- w_out: bfloat16 [8192, 8192], P('head'), may hold values from -0.0625 to 0.0625
Outputs:
- attn_out: bfloat16 [3072, 8192], P(('ctx', 'head'))
The draws below stay inside these ranges and needn't reach their ends.
All inputs are finite; a program needn't handle non-finite values. No bound on the sum of `gate_mask` on one device may be relied on, other than what follows from the above.
Results may differ from the reference program's by a relative error of at most 0.01.
Values may be sent and summed in bfloat16 or wider, within the bound.
A program may use at most 128 MiB of HBM per device.

```python
import jax
import jax.numpy as jnp
from jax import lax

D = 8192
QH = 64
KVH = 8
HD = 128
SINK = 128
WINDOW = 256
SEQ = 3072
N_HEAD = 4


def query_key_pair(key):
    base = jax.random.fold_in(key, 4242)
    query_key, key_key = jax.random.split(base, 2)
    query_data = 2.0 * jnp.clip(jax.random.normal(query_key, (SEQ, QH * HD), jnp.float32), -4.0, 4.0)
    key_data = jnp.clip(jax.random.normal(key_key, (SEQ, KVH * HD), jnp.float32), -4.0, 4.0)
    return (query_data, key_data)


def draw_queries(key, part):
    return query_key_pair(key)[0].astype(jnp.bfloat16)


def draw_keys(key, part):
    return query_key_pair(key)[1].astype(jnp.bfloat16)


def set_ends(drawn, own_key, smallest, top_value):
    shape = drawn.shape
    spot = [jax.random.randint(jax.random.fold_in(own_key, axis), (), 0, shape[axis]) for axis in range(len(shape))]
    drawn = drawn.at[tuple(spot)].set(smallest)
    longest = shape.index(max(shape))
    spot[longest] = (spot[longest] + 1) % shape[longest]
    return drawn.at[tuple(spot)].set(top_value)


def shard_levels(rng, dims, pieces, low, largest):
    gain = 1.0
    for axis_at, parts in pieces:
        heights = jax.random.uniform(jax.random.fold_in(jax.random.fold_in(rng, 6), axis_at), (parts,), jnp.float32, low / len(pieces), largest / len(pieces))
        gain = gain * jnp.repeat(jnp.exp(heights), dims[axis_at] // parts).reshape((-1,) + (1,) * (len(dims) - 1 - axis_at))
    return gain


def centred(key, shape, deviation, bound, cuts=(), kind=jnp.bfloat16):
    level = shard_levels(key, shape, cuts, -0.22, 0.18) if cuts else 1.0
    array = jax.random.normal(key, shape, jnp.float32) * deviation * level
    return jnp.minimum(jnp.maximum(array, -bound), bound).astype(kind)


def setup_inputs(seed: int = 0) -> dict:
    arg_keys = jax.random.split(jax.random.key(seed), 6)
    queries = draw_queries(jax.random.fold_in(arg_keys[5], 71), 0)
    keys = draw_keys(jax.random.fold_in(arg_keys[5], 71), 0)
    values = centred(arg_keys[2], (SEQ, KVH * HD), 4.0, 16.0, ((0, 8), (1, 4)))
    gate_mask = set_ends((jax.random.randint(arg_keys[3], (QH,), 0, 2) < 1).astype(jnp.int32), jax.random.fold_in(arg_keys[3], 1), 0, 1)
    w_out = centred(arg_keys[4], (QH * HD, D), (QH * HD) ** -0.5, 0.0625, ((0, 4),))
    return dict(queries=queries, keys=keys, values=values, gate_mask=gate_mask, w_out=w_out)


def reference(queries, keys, values, gate_mask, w_out):
    repeats = QH // KVH
    score_scale = HD ** -0.5
    positions = jnp.arange(SEQ, dtype=jnp.int32)
    causal = positions[None, :] <= positions[:, None]
    running = causal & ((positions[None, :] > positions[:, None] - WINDOW) | (positions[None, :] < SINK))

    def one_head(operands):
        head_index, gate_value = operands
        group_index = head_index // repeats
        query_cols = lax.dynamic_slice_in_dim(queries, (head_index * HD).astype(jnp.int32), HD, 1)
        key_cols = lax.dynamic_slice_in_dim(keys, (group_index * HD).astype(jnp.int32), HD, 1)
        value_cols = lax.dynamic_slice_in_dim(values, (group_index * HD).astype(jnp.int32), HD, 1)
        scores = jnp.dot(query_cols, key_cols.T, preferred_element_type=jnp.float32) * score_scale

        def attend(allowed):
            masked_scores = jnp.where(allowed, scores, -1e30)
            row_max = jnp.max(masked_scores, axis=1, keepdims=True)
            weights = jnp.where(allowed, jnp.exp(masked_scores - row_max), 0.0)
            weight_sum = jnp.sum(weights, axis=1, keepdims=True)
            return jnp.dot(weights.astype(jnp.bfloat16), value_cols, preferred_element_type=jnp.float32) / weight_sum

        full_out = attend(causal)
        stream_out = attend(running)
        return jnp.where(gate_value == 1, full_out, stream_out).astype(jnp.bfloat16)

    mixed = lax.map(one_head, (jnp.arange(QH, dtype=jnp.int32), gate_mask))
    mixed = jnp.transpose(mixed, (1, 0, 2)).reshape(SEQ, QH * HD)
    group_cols = QH * HD // N_HEAD
    total = jnp.zeros((SEQ, D), jnp.float32)
    for group in range(N_HEAD):
        partial_value = jnp.dot(mixed[:, group * group_cols:(group + 1) * group_cols], w_out[group * group_cols:(group + 1) * group_cols], preferred_element_type=jnp.float32)
        rounded = lax.optimization_barrier(partial_value.astype(jnp.bfloat16))
        total = total + rounded.astype(jnp.float32)
    return total.astype(jnp.bfloat16)
```

```python
import functools

import jax
import jax.numpy as jnp
from jax import lax
from jax.experimental import pallas as pl
from jax.experimental.pallas import tpu as pltpu
from jax.sharding import PartitionSpec as P

HD = 128
SINK = 128
WINDOW = 256
NEG = -1e30
LOG2E = 1.4426950408889634
MESH = pl.DeviceIdType.MESH


def chunk_order(peers):
    return [sorted(range(peers), key=lambda r: (-abs(r - z), -r if z < peers / 2 else r)) for z in range(peers)]


def pick(table, row, step):
    value = jnp.int32(0)
    for z, entries in enumerate(table):
        for s, entry in enumerate(entries):
            value = value + jnp.where((row == z) & (step == s), entry, 0)
    return value


def kernel(
    C, H, G, R, T, NP, D,
    gate_ref, q_ref, k_ref, v_ref, w_ref, out_ref,
    kv, w, part, ng_ref, m_ref, l_ref, acc_ref, mixed, tmp,
    w_sem, k_recv, k_send, k_fwd, p_send, p_recv,
):
    c = lax.axis_index("ctx")
    z = lax.axis_index("head")
    p, k = c // 2, c % 2
    sibling = 2 * p + 1 - k
    chips = C // 2
    rows = T // H
    cols = D // NP

    def w_copy(n):
        return pltpu.make_async_copy(w_ref.at[:, pl.ds(n * cols, cols)], w.at[n], w_sem.at[n])

    for n in range(NP):
        w_copy(n).start()

    for g in range(G):
        kv[c, 0, g] = k_ref[:, g * HD : (g + 1) * HD]
        kv[c, 1, g] = v_ref[:, g * HD : (g + 1) * HD]

    barrier = pltpu.get_barrier_semaphore()
    for q in range(chips):
        @pl.when(q != p)
        def _():
            pl.semaphore_signal(barrier, inc=1, device_id={"ctx": 2 * q + k}, device_id_type=MESH)
    pl.semaphore_signal(barrier, inc=1, device_id={"ctx": sibling}, device_id_type=MESH)

    @pl.when(z > 0)
    def _():
        pl.semaphore_signal(barrier, inc=1, device_id={"head": z - 1}, device_id_type=MESH)

    @pl.when(z < H - 1)
    def _():
        pl.semaphore_signal(barrier, inc=1, device_id={"head": z + 1}, device_id_type=MESH)

    greeted = chips + jnp.where(z > 0, 1, 0) + jnp.where(z < H - 1, 1, 0)
    pl.semaphore_wait(barrier, greeted)

    def kv_copy(block, send, target):
        return pltpu.make_async_remote_copy(
            src_ref=kv.at[block], dst_ref=kv.at[block], send_sem=send, recv_sem=k_recv.at[block],
            device_id={"ctx": target}, device_id_type=MESH,
        )

    for q in reversed(range(chips)):
        @pl.when(q > p)
        def _():
            kv_copy(c, k_send.at[q], 2 * q + k).start()

    @pl.when(k == 0)
    def _():
        kv_copy(c, k_send.at[p], sibling).start()

    for h in range(G * R):
        off = jnp.where(gate_ref[h] == 1, 0.0, 1.0)
        ng_ref[h] = jnp.full((rows, HD), off, jnp.float32)

    scale = HD ** -0.5 * LOG2E

    def attend(g, r, b, kind):
        start = pl.multiple_of(r * rows, rows)
        q = jnp.concatenate(
            [q_ref[pl.ds(start, rows), (g * R + h) * HD : (g * R + h + 1) * HD] for h in range(R)], axis=0
        )
        s = lax.dot_general(
            q, kv[b, 0, g], (((1,), (1,)), ((), ())), preferred_element_type=jnp.float32
        ).reshape(R, rows, T)
        off = ng_ref[g * R : (g + 1) * R, :, 0:1]
        if kind != "middle":
            key_col = lax.broadcasted_iota(jnp.int32, (rows, T), 1)
            ahead = (c - b) * T + start + lax.broadcasted_iota(jnp.int32, (rows, T), 0) - key_col
            near = (ahead < WINDOW) | (b * T + key_col < SINK)
            full_bias = jnp.where(ahead >= 0, 0.0, NEG)
            stream_bias = jnp.where(near, 0.0, NEG) + full_bias
            s = s + jnp.where(off > 0.5, stream_bias[None], full_bias[None])
            top = jnp.max(s, axis=-1, keepdims=True)
            shift = 0.0
        else:
            shift = off * -NEG
            top = jnp.max(s, axis=-1, keepdims=True) - shift
        if kind == "own":
            new = top
        else:
            old = m_ref[g, :, :, 0:1]
            new = jnp.maximum(old, top)
            alpha = jnp.exp2((old - new) * scale)
        e = jnp.exp2(s * scale - (new * scale + shift))
        total = e[:, :, 0:HD]
        for i in range(1, T // HD):
            total = total + e[:, :, i * HD : (i + 1) * HD]
        pv = jnp.dot(
            e.reshape(R * rows, T).astype(jnp.bfloat16), kv[b, 1, g], preferred_element_type=jnp.float32
        ).reshape(R, rows, HD)
        m_ref[g] = jnp.broadcast_to(new, (R, rows, HD))
        if kind == "own":
            l_ref[g] = total
            acc_ref[g] = pv
        else:
            l_ref[g] = l_ref[g] * alpha + total
            acc_ref[g] = acc_ref[g] * alpha + pv

    table = chunk_order(H)

    def part_copy(r, n):
        target = jnp.where(r > z, z + 1, z - 1)
        slot = jnp.where(r == z - 1, H, r)
        return pltpu.make_async_remote_copy(
            src_ref=part.at[r, n], dst_ref=part.at[slot, n],
            send_sem=p_send.at[r, n], recv_sem=p_recv.at[slot, n],
            device_id={"head": target}, device_id_type=MESH,
        )

    def part_wait(slot, n):
        pltpu.make_async_remote_copy(
            src_ref=part.at[slot, n], dst_ref=part.at[slot, n],
            send_sem=p_send.at[0, n], recv_sem=p_recv.at[slot, n],
            device_id={"ctx": sibling}, device_id_type=MESH,
        ).wait_recv()

    def chunk(step, carry):
        r = pick(table, z, step)
        for g in range(G):
            attend(g, r, c, "own")

        def one_block(j, inner):
            rest = j - k
            odd = rest % 2
            lead = (k == 1) & (j == 0)
            b = jnp.where(lead, c - 1, 2 * (p - 1 - rest // 2) + jnp.where(odd == 0, k, 1 - k))
            b = jnp.where(b < 0, 0, b)

            @pl.when(step == 0)
            def _():
                kv_copy(b, k_send.at[0], sibling).wait_recv()

                @pl.when(jnp.logical_not(lead) & (odd == 0))
                def _():
                    kv_copy(b, k_fwd.at[b // 2], sibling).start()

            edge = (b == c - 1) | (b == 0)

            @pl.when(edge)
            def _():
                for g in range(G):
                    attend(g, r, b, "edge")

            @pl.when(jnp.logical_not(edge))
            def _():
                for g in range(G):
                    attend(g, r, b, "middle")

            return inner

        lax.fori_loop(0, c, one_block, 0)
        for g in range(G):
            o = acc_ref[g] / jnp.sum(l_ref[g], axis=-1, keepdims=True)
            for h in range(R):
                mixed[:, (g * R + h) * HD : (g * R + h + 1) * HD] = o[h].astype(jnp.bfloat16)

        has_a = ((r > z) & (z > 0)) | ((r < z) & (z < H - 1)) | ((r == z) & (z > 0))
        has_b = (r == z) & (z < H - 1)

        def piece(n, inner):
            @pl.when(step == 0)
            def _():
                w_copy(n).wait()

            tmp[...] = jnp.dot(mixed[...], w[n], preferred_element_type=jnp.float32)

            @pl.when(has_a)
            def _():
                part_wait(r, n)
                tmp[...] += part[r, n].astype(jnp.float32)

            @pl.when(has_b)
            def _():
                part_wait(H, n)
                tmp[...] += part[H, n].astype(jnp.float32)

            @pl.when(r == z)
            def _():
                out_ref[:, pl.ds(pl.multiple_of(n * cols, cols), cols)] = tmp[...].astype(jnp.bfloat16)

            @pl.when(r != z)
            def _():
                part[r, n] = tmp[...].astype(jnp.bfloat16)
                part_copy(r, n).start()

            return inner

        lax.fori_loop(0, NP, piece, 0)
        return carry

    lax.fori_loop(0, H, chunk, 0)

    for q in range(chips):
        @pl.when(q > p)
        def _():
            kv_copy(c, k_send.at[q], 2 * q + k).wait_send()

        @pl.when(q < p)
        def _():
            kv_copy(2 * q + k, k_fwd.at[q], sibling).wait_send()

    @pl.when(k == 0)
    def _():
        kv_copy(c, k_send.at[p], sibling).wait_send()

    def drain(i, carry):
        @pl.when(i // NP != z)
        def _():
            part_copy(i // NP, i % NP).wait_send()

        return carry

    lax.fori_loop(0, H * NP, drain, 0)


def solution(mesh):
    C, H = mesh.shape["ctx"], mesh.shape["head"]

    def shards(queries, keys, values, gate_mask, w_out):
        T = queries.shape[0]
        G = keys.shape[1] // HD
        R = queries.shape[1] // keys.shape[1]
        K, D = w_out.shape
        rows = T // H
        NP = 8
        vmem = pl.BlockSpec(memory_space=pltpu.VMEM)
        return pl.pallas_call(
            functools.partial(kernel, C, H, G, R, T, NP, D),
            out_shape=jax.ShapeDtypeStruct((rows, D), jnp.bfloat16),
            in_specs=[pl.BlockSpec(memory_space=pltpu.SMEM), vmem, vmem, vmem, pl.BlockSpec(memory_space=pl.ANY)],
            out_specs=vmem,
            scratch_shapes=[
                pltpu.VMEM((C, 2, G, T, HD), jnp.bfloat16),
                pltpu.VMEM((NP, K, D // NP), jnp.bfloat16),
                pltpu.VMEM((H + 1, NP, rows, D // NP), jnp.bfloat16),
                pltpu.VMEM((G * R, rows, HD), jnp.float32),
                pltpu.VMEM((G, R, rows, HD), jnp.float32),
                pltpu.VMEM((G, R, rows, HD), jnp.float32),
                pltpu.VMEM((G, R, rows, HD), jnp.float32),
                pltpu.VMEM((rows, K), jnp.bfloat16),
                pltpu.VMEM((rows, D // NP), jnp.float32),
                pltpu.SemaphoreType.DMA((NP,)),
                pltpu.SemaphoreType.DMA((C,)),
                pltpu.SemaphoreType.DMA((C // 2,)),
                pltpu.SemaphoreType.DMA((C // 2,)),
                pltpu.SemaphoreType.DMA((H, NP)),
                pltpu.SemaphoreType.DMA((H + 1, NP)),
            ],
            compiler_params=pltpu.CompilerParams(
                collective_id=0, has_side_effects=True, vmem_limit_bytes=60 * 2**20
            ),
        )(gate_mask, queries, keys, values, w_out)

    in_specs = (P("ctx", "head"), P("ctx", "head"), P("ctx", "head"), P("head"), P("head", None))
    out_specs = P(("ctx", "head"), None)
    return jax.shard_map(shards, mesh=mesh, in_specs=in_specs, out_specs=out_specs, check_vma=False)
```

```python
import functools

import jax
import jax.numpy as jnp
from jax import lax
from jax.experimental import pallas as pl
from jax.experimental.pallas import tpu as pltpu
from jax.sharding import PartitionSpec as P

HD = 128
SINK = 128
WINDOW = 256
NEG = -1e30
LOG2E = 1.4426950408889634
MESH = pl.DeviceIdType.MESH


def chunk_order(peers):
    return [sorted(range(peers), key=lambda r: (-abs(r - z), -r if z < peers / 2 else r)) for z in range(peers)]


def pick(table, row, step):
    value = jnp.int32(0)
    for z, entries in enumerate(table):
        for s, entry in enumerate(entries):
            value = value + jnp.where((row == z) & (step == s), entry, 0)
    return value


def kernel(
    C, H, G, R, T, NP, D,
    gate_ref, q_ref, k_ref, v_ref, w_ref, out_ref,
    kv, w, part, ng_ref, m_ref, l_ref, acc_ref, mixed, tmp,
    w_sem, k_recv, k_send, k_fwd, p_send, p_recv,
):
    c = lax.axis_index("ctx")
    z = lax.axis_index("head")
    p, k = c // 2, c % 2
    sibling = 2 * p + 1 - k
    chips = C // 2
    rows = T // H
    cols = D // NP

    def w_copy(n):
        return pltpu.make_async_copy(w_ref.at[:, pl.ds(n * cols, cols)], w.at[n], w_sem.at[n])

    for g in range(G):
        kv[c, 0, g] = k_ref[:, g * HD : (g + 1) * HD]
        kv[c, 1, g] = v_ref[:, g * HD : (g + 1) * HD]

    barrier = pltpu.get_barrier_semaphore()
    for q in range(chips):
        @pl.when(q != p)
        def _():
            pl.semaphore_signal(barrier, inc=1, device_id={"ctx": 2 * q + k}, device_id_type=MESH)
    pl.semaphore_signal(barrier, inc=1, device_id={"ctx": sibling}, device_id_type=MESH)

    @pl.when(z > 0)
    def _():
        pl.semaphore_signal(barrier, inc=1, device_id={"head": z - 1}, device_id_type=MESH)

    @pl.when(z < H - 1)
    def _():
        pl.semaphore_signal(barrier, inc=1, device_id={"head": z + 1}, device_id_type=MESH)

    greeted = chips + jnp.where(z > 0, 1, 0) + jnp.where(z < H - 1, 1, 0)
    pl.semaphore_wait(barrier, greeted)

    def kv_copy(block, send, target):
        return pltpu.make_async_remote_copy(
            src_ref=kv.at[block], dst_ref=kv.at[block], send_sem=send, recv_sem=k_recv.at[block],
            device_id={"ctx": target}, device_id_type=MESH,
        )

    for q in reversed(range(chips)):
        @pl.when(q > p)
        def _():
            kv_copy(c, k_send.at[q], 2 * q + k).start()

    @pl.when(k == 0)
    def _():
        kv_copy(c, k_send.at[p], sibling).start()

    for n in range(NP):
        w_copy(n).start()

    for h in range(G * R):
        off = jnp.where(gate_ref[h] == 1, 0.0, NEG)
        ng_ref[h] = jnp.full((rows, HD), off, jnp.float32)

    scale = HD ** -0.5 * LOG2E

    def attend(g, r, b, kind):
        start = pl.multiple_of(r * rows, rows)
        q = jnp.concatenate(
            [q_ref[pl.ds(start, rows), (g * R + h) * HD : (g * R + h + 1) * HD] for h in range(R)], axis=0
        )
        s = lax.dot_general(
            q, kv[b, 0, g], (((1,), (1,)), ((), ())), preferred_element_type=jnp.float32
        ).reshape(R, rows, T)
        tiles = [s[:, :, i * HD : (i + 1) * HD] for i in range(T // HD)]
        off = ng_ref[g * R : (g + 1) * R]
        if kind != "middle":
            row_pos = (c - b) * T + start + lax.broadcasted_iota(jnp.int32, (rows, HD), 0)
            for i in range(T // HD):
                key_col = i * HD + lax.broadcasted_iota(jnp.int32, (rows, HD), 1)
                ahead = row_pos - key_col
                near = (ahead < WINDOW) | (b * T + key_col < SINK)
                tiles[i] = tiles[i] + jnp.maximum(jnp.where(near, 0.0, NEG)[None], off)
                if kind == "own":
                    tiles[i] = tiles[i] + jnp.where(ahead >= 0, 0.0, NEG)[None]
        top = tiles[0]
        for tile in tiles[1:]:
            top = jnp.maximum(top, tile)
        top = jnp.broadcast_to(jnp.max(top, axis=-1, keepdims=True), top.shape)
        if kind == "middle":
            top = top + off
        if kind == "own":
            new = top
        else:
            old = m_ref[g]
            new = jnp.maximum(old, top)
            alpha = jnp.exp2((old - new) * scale)
        shift = new * scale
        if kind == "middle":
            shift = shift - off
        e = [jnp.exp2(tile * scale - shift) for tile in tiles]
        total = e[0]
        for tile in e[1:]:
            total = total + tile
        weights = jnp.concatenate([tile.astype(jnp.bfloat16) for tile in e], axis=-1).reshape(R * rows, T)
        pv = jnp.dot(weights, kv[b, 1, g], preferred_element_type=jnp.float32).reshape(R, rows, HD)
        m_ref[g] = new
        if kind == "own":
            l_ref[g] = total
            acc_ref[g] = pv
        else:
            l_ref[g] = l_ref[g] * alpha + total
            acc_ref[g] = acc_ref[g] * alpha + pv

    table = chunk_order(H)

    def part_copy(r, n):
        target = jnp.where(r > z, z + 1, z - 1)
        slot = jnp.where(r == z - 1, H, r)
        return pltpu.make_async_remote_copy(
            src_ref=part.at[r, n], dst_ref=part.at[slot, n],
            send_sem=p_send.at[r, n], recv_sem=p_recv.at[slot, n],
            device_id={"head": target}, device_id_type=MESH,
        )

    def part_wait(slot, n):
        pltpu.make_async_remote_copy(
            src_ref=part.at[slot, n], dst_ref=part.at[slot, n],
            send_sem=p_send.at[0, n], recv_sem=p_recv.at[slot, n],
            device_id={"ctx": sibling}, device_id_type=MESH,
        ).wait_recv()

    def chunk(step, carry):
        r = pick(table, z, step)
        for g in range(G):
            attend(g, r, c, "own")

        def one_block(j, inner):
            rest = j - k
            odd = rest % 2
            lead = (k == 1) & (j == 0)
            b = jnp.where(lead, c - 1, 2 * (p - 1 - rest // 2) + jnp.where(odd == 0, k, 1 - k))
            b = jnp.where(b < 0, 0, b)

            @pl.when(step == 0)
            def _():
                kv_copy(b, k_send.at[0], sibling).wait_recv()

                @pl.when(jnp.logical_not(lead) & (odd == 0))
                def _():
                    kv_copy(b, k_fwd.at[b // 2], sibling).start()

            edge = (b == c - 1) | (b == 0)

            @pl.when(edge)
            def _():
                for g in range(G):
                    attend(g, r, b, "edge")

            @pl.when(jnp.logical_not(edge))
            def _():
                for g in range(G):
                    attend(g, r, b, "middle")

            return inner

        lax.fori_loop(0, c, one_block, 0)
        for g in range(G):
            o = acc_ref[g] / jnp.sum(l_ref[g], axis=-1, keepdims=True)
            for h in range(R):
                mixed[:, (g * R + h) * HD : (g * R + h + 1) * HD] = o[h].astype(jnp.bfloat16)

        has_a = ((r > z) & (z > 0)) | ((r < z) & (z < H - 1)) | ((r == z) & (z > 0))
        has_b = (r == z) & (z < H - 1)

        def piece(n, inner):
            @pl.when(step == 0)
            def _():
                w_copy(n).wait()

            tmp[...] = jnp.dot(mixed[...], w[n], preferred_element_type=jnp.float32)

            @pl.when(has_a)
            def _():
                part_wait(r, n)
                tmp[...] += part[r, n].astype(jnp.float32)

            @pl.when(has_b)
            def _():
                part_wait(H, n)
                tmp[...] += part[H, n].astype(jnp.float32)

            @pl.when(r == z)
            def _():
                out_ref[:, pl.ds(pl.multiple_of(n * cols, cols), cols)] = tmp[...].astype(jnp.bfloat16)

            @pl.when(r != z)
            def _():
                part[r, n] = tmp[...].astype(jnp.bfloat16)
                part_copy(r, n).start()

            return inner

        lax.fori_loop(0, NP, piece, 0)
        return carry

    lax.fori_loop(0, H, chunk, 0)

    for q in range(chips):
        @pl.when(q > p)
        def _():
            kv_copy(c, k_send.at[q], 2 * q + k).wait_send()

        @pl.when(q < p)
        def _():
            kv_copy(2 * q + k, k_fwd.at[q], sibling).wait_send()

    @pl.when(k == 0)
    def _():
        kv_copy(c, k_send.at[p], sibling).wait_send()

    def drain(i, carry):
        @pl.when(i // NP != z)
        def _():
            part_copy(i // NP, i % NP).wait_send()

        return carry

    lax.fori_loop(0, H * NP, drain, 0)


def solution(mesh):
    C, H = mesh.shape["ctx"], mesh.shape["head"]

    def shards(queries, keys, values, gate_mask, w_out):
        T = queries.shape[0]
        G = keys.shape[1] // HD
        R = queries.shape[1] // keys.shape[1]
        K, D = w_out.shape
        rows = T // H
        NP = 8
        vmem = pl.BlockSpec(memory_space=pltpu.VMEM)
        return pl.pallas_call(
            functools.partial(kernel, C, H, G, R, T, NP, D),
            out_shape=jax.ShapeDtypeStruct((rows, D), jnp.bfloat16),
            in_specs=[pl.BlockSpec(memory_space=pltpu.SMEM), vmem, vmem, vmem, pl.BlockSpec(memory_space=pl.ANY)],
            out_specs=vmem,
            scratch_shapes=[
                pltpu.VMEM((C, 2, G, T, HD), jnp.bfloat16),
                pltpu.VMEM((NP, K, D // NP), jnp.bfloat16),
                pltpu.VMEM((H + 1, NP, rows, D // NP), jnp.bfloat16),
                pltpu.VMEM((G * R, rows, HD), jnp.float32),
                pltpu.VMEM((G, R, rows, HD), jnp.float32),
                pltpu.VMEM((G, R, rows, HD), jnp.float32),
                pltpu.VMEM((G, R, rows, HD), jnp.float32),
                pltpu.VMEM((rows, K), jnp.bfloat16),
                pltpu.VMEM((rows, D // NP), jnp.float32),
                pltpu.SemaphoreType.DMA((NP,)),
                pltpu.SemaphoreType.DMA((C,)),
                pltpu.SemaphoreType.DMA((C // 2,)),
                pltpu.SemaphoreType.DMA((C // 2,)),
                pltpu.SemaphoreType.DMA((H, NP)),
                pltpu.SemaphoreType.DMA((H + 1, NP)),
            ],
            compiler_params=pltpu.CompilerParams(
                collective_id=0, has_side_effects=True, vmem_limit_bytes=60 * 2**20
            ),
        )(gate_mask, queries, keys, values, w_out)

    in_specs = (P("ctx", "head"), P("ctx", "head"), P("ctx", "head"), P("head"), P("head", None))
    out_specs = P(("ctx", "head"), None)
    return jax.shard_map(shards, mesh=mesh, in_specs=in_specs, out_specs=out_specs, check_vma=False)
```

```python
import functools

import jax
import jax.numpy as jnp
from jax import lax
from jax.experimental import pallas as pl
from jax.experimental.pallas import tpu as pltpu
from jax.sharding import PartitionSpec as P

HD = 128
SINK = 128
WINDOW = 256
NEG = -1e30
LOG2E = 1.4426950408889634
MESH = pl.DeviceIdType.MESH


def chunk_order(peers):
    return [sorted(range(peers), key=lambda r: (-abs(r - z), -r if z < peers / 2 else r)) for z in range(peers)]


def pick(table, row, step):
    value = jnp.int32(0)
    for z, entries in enumerate(table):
        for s, entry in enumerate(entries):
            value = value + jnp.where((row == z) & (step == s), entry, 0)
    return value


def kernel(
    C, H, G, R, T, NP, D,
    gate_ref, q_hbm, k_ref, v_ref, w_ref, out_hbm,
    q_ref, out_ref, kv, w, part, ng_ref, m_ref, l_ref, acc_ref, mixed, tmp,
    q_sem, kv_sem, out_sem, w_sem, k_recv, k_send, k_fwd, k_relay, p_send, p_recv,
):
    c = lax.axis_index("ctx")
    z = lax.axis_index("head")
    p, k = c // 2, c % 2
    sibling = 2 * p + 1 - k
    chips = C // 2
    rows = T // H
    cols = D // NP

    def w_copy(n):
        return pltpu.make_async_copy(w_ref.at[:, pl.ds(n * cols, cols)], w.at[n], w_sem.at[n])

    own_copies = []
    for g in range(G):
        for i, source in enumerate((k_ref, v_ref)):
            own_copies.append(
                pltpu.make_async_copy(source.at[:, pl.ds(g * HD, HD)], kv.at[c, g, i], kv_sem.at[i, g])
            )
    q_copy = pltpu.make_async_copy(q_hbm, q_ref, q_sem)
    for copy in own_copies:
        copy.start()
    q_copy.start()

    barrier = pltpu.get_barrier_semaphore()
    for q in range(chips):
        @pl.when(q != p)
        def _():
            pl.semaphore_signal(barrier, inc=1, device_id={"ctx": 2 * q + k}, device_id_type=MESH)
    pl.semaphore_signal(barrier, inc=1, device_id={"ctx": sibling}, device_id_type=MESH)

    @pl.when(z > 0)
    def _():
        pl.semaphore_signal(barrier, inc=1, device_id={"head": z - 1}, device_id_type=MESH)

    @pl.when(z < H - 1)
    def _():
        pl.semaphore_signal(barrier, inc=1, device_id={"head": z + 1}, device_id_type=MESH)

    greeted = chips + jnp.where(z > 0, 1, 0) + jnp.where(z < H - 1, 1, 0)
    pl.semaphore_wait(barrier, greeted)

    for copy in own_copies:
        copy.wait()

    def kv_copy(block, g, send, target):
        return pltpu.make_async_remote_copy(
            src_ref=kv.at[block, g], dst_ref=kv.at[block, g], send_sem=send.at[g], recv_sem=k_recv.at[block, g],
            device_id={"ctx": target}, device_id_type=MESH,
        )

    relays = chips == 4

    def pushes(q):
        return (q > p) & (q + p != chips - 1) if relays else q > p

    for g in range(G):
        for q in reversed(range(chips)):
            @pl.when(pushes(q))
            def _():
                kv_copy(c, g, k_send.at[q], 2 * q + k).start()

        @pl.when(k == 0)
        def _():
            kv_copy(c, g, k_send.at[p], sibling).start()

    for n in range(NP):
        w_copy(n).start()

    for h in range(G * R):
        off = jnp.where(gate_ref[h] == 1, 0.0, NEG)
        ng_ref[h] = jnp.full((rows, HD), off, jnp.float32)

    q_copy.wait()
    scale = HD ** -0.5 * LOG2E

    def attend(g, r, b, kind):
        start = pl.multiple_of(r * rows, rows)
        q = jnp.concatenate(
            [q_ref[pl.ds(start, rows), (g * R + h) * HD : (g * R + h + 1) * HD] for h in range(R)], axis=0
        )
        s = lax.dot_general(
            q, kv[b, g, 0], (((1,), (1,)), ((), ())), preferred_element_type=jnp.float32
        ).reshape(R, rows, T)
        tiles = [s[:, :, i * HD : (i + 1) * HD] for i in range(T // HD)]
        off = ng_ref[g * R : (g + 1) * R]
        if kind != "middle":
            row_pos = (c - b) * T + start + lax.broadcasted_iota(jnp.int32, (rows, HD), 0)
            for i in range(T // HD):
                key_col = i * HD + lax.broadcasted_iota(jnp.int32, (rows, HD), 1)
                ahead = row_pos - key_col
                near = (ahead < WINDOW) | (b * T + key_col < SINK)
                tiles[i] = tiles[i] + jnp.maximum(jnp.where(near, 0.0, NEG)[None], off)
                if kind == "own":
                    tiles[i] = tiles[i] + jnp.where(ahead >= 0, 0.0, NEG)[None]
        top = tiles[0]
        for tile in tiles[1:]:
            top = jnp.maximum(top, tile)
        top = jnp.broadcast_to(jnp.max(top, axis=-1, keepdims=True), top.shape)
        if kind == "middle":
            top = top + off
        if kind == "own":
            new = top
        else:
            old = m_ref[g]
            new = jnp.maximum(old, top)
            alpha = jnp.exp2((old - new) * scale)
        shift = new * scale
        if kind == "middle":
            shift = shift - off
        e = [jnp.exp2(tile * scale - shift) for tile in tiles]
        total = e[0]
        for tile in e[1:]:
            total = total + tile
        weights = jnp.concatenate([tile.astype(jnp.bfloat16) for tile in e], axis=-1).reshape(R * rows, T)
        pv = jnp.dot(weights, kv[b, g, 1], preferred_element_type=jnp.float32).reshape(R, rows, HD)
        m_ref[g] = new
        if kind == "own":
            l_ref[g] = total
            acc_ref[g] = pv
        else:
            l_ref[g] = l_ref[g] * alpha + total
            acc_ref[g] = acc_ref[g] * alpha + pv

    table = chunk_order(H)
    relay_target = jnp.where(p == 3, 4, 6) + k

    def out_copy(n):
        place = pl.ds(pl.multiple_of(n * cols, cols), cols)
        return pltpu.make_async_copy(out_ref.at[n], out_hbm.at[:, place], out_sem.at[n])

    def part_copy(r, n):
        target = jnp.where(r > z, z + 1, z - 1)
        slot = jnp.where(r == z - 1, H, r)
        return pltpu.make_async_remote_copy(
            src_ref=part.at[r, n], dst_ref=part.at[slot, n],
            send_sem=p_send.at[r, n], recv_sem=p_recv.at[slot, n],
            device_id={"head": target}, device_id_type=MESH,
        )

    def part_wait(slot, n):
        pltpu.make_async_remote_copy(
            src_ref=part.at[slot, n], dst_ref=part.at[slot, n],
            send_sem=p_send.at[0, n], recv_sem=p_recv.at[slot, n],
            device_id={"ctx": sibling}, device_id_type=MESH,
        ).wait_recv()

    def chunk(step, carry):
        r = pick(table, z, step)
        for g in range(G):
            attend(g, r, c, "own")

        def one_block(j, inner):
            rest = j - k
            odd = rest % 2
            lead = (k == 1) & (j == 0)
            turn = rest // 2
            from_chip = p - 1 - turn
            if relays:
                from_chip = jnp.where(p == 2, turn, jnp.where((p == 3) & (turn < 2), 1 + turn, from_chip))
            b = jnp.where(lead, c - 1, 2 * from_chip + jnp.where(odd == 0, k, 1 - k))
            b = jnp.where(b < 0, 0, b)

            @pl.when(step == 0)
            def _():
                for g in range(G):
                    kv_copy(b, g, k_send.at[0], sibling).wait_recv()

                    if relays:
                        @pl.when(((p == 1 + k) & (b == k)) | ((p == 3) & (b == 2 + k)))
                        def _():
                            kv_copy(b, g, k_relay, relay_target).start()

                    @pl.when(jnp.logical_not(lead) & (odd == 0))
                    def _():
                        kv_copy(b, g, k_fwd.at[b // 2], sibling).start()

            edge = (b == c - 1) | (b == 0)

            @pl.when(edge)
            def _():
                for g in range(G):
                    attend(g, r, b, "edge")

            @pl.when(jnp.logical_not(edge))
            def _():
                for g in range(G):
                    attend(g, r, b, "middle")

            return inner

        lax.fori_loop(0, c, one_block, 0)
        for g in range(G):
            o = acc_ref[g] / jnp.sum(l_ref[g], axis=-1, keepdims=True)
            for h in range(R):
                mixed[:, (g * R + h) * HD : (g * R + h + 1) * HD] = o[h].astype(jnp.bfloat16)

        has_a = ((r > z) & (z > 0)) | ((r < z) & (z < H - 1)) | ((r == z) & (z > 0))
        has_b = (r == z) & (z < H - 1)

        def piece(n, inner):
            @pl.when(step == 0)
            def _():
                w_copy(n).wait()

            tmp[...] = jnp.dot(mixed[...], w[n], preferred_element_type=jnp.float32)

            @pl.when(has_a)
            def _():
                part_wait(r, n)
                tmp[...] += part[r, n].astype(jnp.float32)

            @pl.when(has_b)
            def _():
                part_wait(H, n)
                tmp[...] += part[H, n].astype(jnp.float32)

            @pl.when(r == z)
            def _():
                out_ref[n] = tmp[...].astype(jnp.bfloat16)
                out_copy(n).start()

            @pl.when(r != z)
            def _():
                part[r, n] = tmp[...].astype(jnp.bfloat16)
                part_copy(r, n).start()

            return inner

        lax.fori_loop(0, NP, piece, 0)
        return carry

    lax.fori_loop(0, H, chunk, 0)

    for g in range(G):
        for q in range(chips):
            @pl.when(pushes(q))
            def _():
                kv_copy(c, g, k_send.at[q], 2 * q + k).wait_send()

            @pl.when(q < p)
            def _():
                kv_copy(2 * q + k, g, k_fwd.at[q], sibling).wait_send()

        @pl.when(k == 0)
        def _():
            kv_copy(c, g, k_send.at[p], sibling).wait_send()

        if relays:
            @pl.when((p == 1 + k) | (p == 3))
            def _():
                kv_copy(jnp.where(p == 3, 2 + k, k), g, k_relay, relay_target).wait_send()

    def drain(i, carry):
        @pl.when(i // NP != z)
        def _():
            part_copy(i // NP, i % NP).wait_send()

        return carry

    lax.fori_loop(0, H * NP, drain, 0)
    for n in range(NP):
        out_copy(n).wait()


def solution(mesh):
    C, H = mesh.shape["ctx"], mesh.shape["head"]

    def shards(queries, keys, values, gate_mask, w_out):
        T = queries.shape[0]
        G = keys.shape[1] // HD
        R = queries.shape[1] // keys.shape[1]
        K, D = w_out.shape
        rows = T // H
        NP = 8
        hbm = pl.BlockSpec(memory_space=pl.ANY)
        return pl.pallas_call(
            functools.partial(kernel, C, H, G, R, T, NP, D),
            out_shape=jax.ShapeDtypeStruct((rows, D), jnp.bfloat16),
            in_specs=[pl.BlockSpec(memory_space=pltpu.SMEM), hbm, hbm, hbm, hbm],
            out_specs=hbm,
            scratch_shapes=[
                pltpu.VMEM((T, G * R * HD), jnp.bfloat16),
                pltpu.VMEM((NP, rows, D // NP), jnp.bfloat16),
                pltpu.VMEM((C, G, 2, T, HD), jnp.bfloat16),
                pltpu.VMEM((NP, K, D // NP), jnp.bfloat16),
                pltpu.VMEM((H + 1, NP, rows, D // NP), jnp.bfloat16),
                pltpu.VMEM((G * R, rows, HD), jnp.float32),
                pltpu.VMEM((G, R, rows, HD), jnp.float32),
                pltpu.VMEM((G, R, rows, HD), jnp.float32),
                pltpu.VMEM((G, R, rows, HD), jnp.float32),
                pltpu.VMEM((rows, K), jnp.bfloat16),
                pltpu.VMEM((rows, D // NP), jnp.float32),
                pltpu.SemaphoreType.DMA,
                pltpu.SemaphoreType.DMA((2, G)),
                pltpu.SemaphoreType.DMA((NP,)),
                pltpu.SemaphoreType.DMA((NP,)),
                pltpu.SemaphoreType.DMA((C, G)),
                pltpu.SemaphoreType.DMA((C // 2, G)),
                pltpu.SemaphoreType.DMA((C // 2, G)),
                pltpu.SemaphoreType.DMA((G,)),
                pltpu.SemaphoreType.DMA((H, NP)),
                pltpu.SemaphoreType.DMA((H + 1, NP)),
            ],
            compiler_params=pltpu.CompilerParams(
                collective_id=0, has_side_effects=True, vmem_limit_bytes=60 * 2**20
            ),
        )(gate_mask, queries, keys, values, w_out)

    in_specs = (P("ctx", "head"), P("ctx", "head"), P("ctx", "head"), P("head"), P("head", None))
    out_specs = P(("ctx", "head"), None)
    return jax.shard_map(shards, mesh=mesh, in_specs=in_specs, out_specs=out_specs, check_vma=False)
```

```python
import functools

import jax
import jax.numpy as jnp
from jax import lax
from jax.experimental import pallas as pl
from jax.experimental.pallas import tpu as pltpu
from jax.sharding import PartitionSpec as P

HD = 128
SINK = 128
WINDOW = 256
NEG = -1e30
LOG2E = 1.4426950408889634
MESH = pl.DeviceIdType.MESH


def chunk_order(peers):
    return [sorted(range(peers), key=lambda r: (-abs(r - z), -r if z < peers / 2 else r)) for z in range(peers)]


def pick(table, row, step):
    value = jnp.int32(0)
    for z, entries in enumerate(table):
        for s, entry in enumerate(entries):
            value = value + jnp.where((row == z) & (step == s), entry, 0)
    return value


def kernel(
    C, H, G, R, T, NP, D,
    gate_ref, q_hbm, k_ref, v_ref, w_ref, out_hbm,
    q_ref, out_ref, kv, w, part, ng_ref, m_ref, l_ref, acc_ref, mixed, tmp,
    q_sem, kv_sem, out_sem, w_sem, k_recv, k_send, k_fwd, k_relay, p_send, p_recv,
):
    c = lax.axis_index("ctx")
    z = lax.axis_index("head")
    p, k = c // 2, c % 2
    sibling = 2 * p + 1 - k
    chips = C // 2
    rows = T // H
    cols = D // NP

    def w_copy(n):
        return pltpu.make_async_copy(w_ref.at[:, pl.ds(n * cols, cols)], w.at[n], w_sem.at[n])

    own_copies = []
    for g in range(G):
        for i, source in enumerate((k_ref, v_ref)):
            own_copies.append(
                pltpu.make_async_copy(source.at[:, pl.ds(g * HD, HD)], kv.at[c, g, i], kv_sem.at[i, g])
            )
    q_copy = pltpu.make_async_copy(q_hbm, q_ref, q_sem)
    for copy in own_copies:
        copy.start()
    q_copy.start()

    barrier = pltpu.get_barrier_semaphore()
    for q in range(chips):
        @pl.when(q != p)
        def _():
            pl.semaphore_signal(barrier, inc=1, device_id={"ctx": 2 * q + k}, device_id_type=MESH)
    pl.semaphore_signal(barrier, inc=1, device_id={"ctx": sibling}, device_id_type=MESH)

    @pl.when(z > 0)
    def _():
        pl.semaphore_signal(barrier, inc=1, device_id={"head": z - 1}, device_id_type=MESH)

    @pl.when(z < H - 1)
    def _():
        pl.semaphore_signal(barrier, inc=1, device_id={"head": z + 1}, device_id_type=MESH)

    greeted = chips + jnp.where(z > 0, 1, 0) + jnp.where(z < H - 1, 1, 0)
    pl.semaphore_wait(barrier, greeted)

    for copy in own_copies:
        copy.wait()

    def kv_copy(block, g, send, target):
        return pltpu.make_async_remote_copy(
            src_ref=kv.at[block, g], dst_ref=kv.at[block, g], send_sem=send.at[g], recv_sem=k_recv.at[block, g],
            device_id={"ctx": target}, device_id_type=MESH,
        )

    relays = chips == 4

    def pushes(q):
        return (q > p) & (q + p != chips - 1) if relays else q > p

    for g in range(G):
        for q in reversed(range(chips)):
            @pl.when(pushes(q))
            def _():
                kv_copy(c, g, k_send.at[q], 2 * q + k).start()

        @pl.when(k == 0)
        def _():
            kv_copy(c, g, k_send.at[p], sibling).start()

    for n in range(NP):
        w_copy(n).start()

    for h in range(G * R):
        off = jnp.where(gate_ref[h] == 1, 0.0, NEG)
        ng_ref[h] = jnp.full((rows, HD), off, jnp.float32)

    q_copy.wait()
    scale = HD ** -0.5 * LOG2E

    def attend(g, r, b, kind):
        start = pl.multiple_of(r * rows, rows)
        q = jnp.concatenate(
            [q_ref[pl.ds(start, rows), (g * R + h) * HD : (g * R + h + 1) * HD] for h in range(R)], axis=0
        )
        s = lax.dot_general(
            q, kv[b, g, 0], (((1,), (1,)), ((), ())), preferred_element_type=jnp.float32
        ).reshape(R, rows, T)
        tiles = [s[:, :, i * HD : (i + 1) * HD] for i in range(T // HD)]
        off = ng_ref[g * R : (g + 1) * R]
        if kind != "middle":
            row_pos = (c - b) * T + start + lax.broadcasted_iota(jnp.int32, (rows, HD), 0)
            for i in range(T // HD):
                key_col = i * HD + lax.broadcasted_iota(jnp.int32, (rows, HD), 1)
                ahead = row_pos - key_col
                near = (ahead < WINDOW) | (b * T + key_col < SINK)
                tiles[i] = tiles[i] + jnp.maximum(jnp.where(near, 0.0, NEG)[None], off)
                if kind == "own":
                    tiles[i] = tiles[i] + jnp.where(ahead >= 0, 0.0, NEG)[None]
        top = tiles[0]
        for tile in tiles[1:]:
            top = jnp.maximum(top, tile)
        top = jnp.broadcast_to(jnp.max(top, axis=-1, keepdims=True), top.shape)
        if kind == "middle":
            top = top + off
        if kind == "own":
            new = top
        else:
            old = m_ref[g]
            new = jnp.maximum(old, top)
            alpha = jnp.exp2((old - new) * scale)
        shift = new * scale
        if kind == "middle":
            shift = shift - off
        e = [jnp.exp2(tile * scale - shift) for tile in tiles]
        total = e[0]
        for tile in e[1:]:
            total = total + tile
        weights = jnp.concatenate([tile.astype(jnp.bfloat16) for tile in e], axis=-1).reshape(R * rows, T)
        pv = jnp.dot(weights, kv[b, g, 1], preferred_element_type=jnp.float32).reshape(R, rows, HD)
        m_ref[g] = new
        if kind == "own":
            l_ref[g] = total
            acc_ref[g] = pv
        else:
            l_ref[g] = l_ref[g] * alpha + total
            acc_ref[g] = acc_ref[g] * alpha + pv

    table = chunk_order(H)
    relay_target = jnp.where(p == 3, 4, 6) + k

    def out_copy(n):
        place = pl.ds(pl.multiple_of(n * cols, cols), cols)
        return pltpu.make_async_copy(out_ref.at[n], out_hbm.at[:, place], out_sem.at[n])

    def part_copy(r, n):
        target = jnp.where(r > z, z + 1, z - 1)
        slot = jnp.where(r == z - 1, H, r)
        return pltpu.make_async_remote_copy(
            src_ref=part.at[r, n], dst_ref=part.at[slot, n],
            send_sem=p_send.at[r, n], recv_sem=p_recv.at[slot, n],
            device_id={"head": target}, device_id_type=MESH,
        )

    def part_wait(slot, n):
        pltpu.make_async_remote_copy(
            src_ref=part.at[slot, n], dst_ref=part.at[slot, n],
            send_sem=p_send.at[0, n], recv_sem=p_recv.at[slot, n],
            device_id={"ctx": sibling}, device_id_type=MESH,
        ).wait_recv()

    def chunk(step, carry):
        r = pick(table, z, step)
        for g in range(G):
            attend(g, r, c, "own")

        def one_block(j, inner):
            rest = j - k
            odd = rest % 2
            lead = (k == 1) & (j == 0)
            turn = rest // 2
            from_chip = p - 1 - turn
            if relays:
                from_chip = jnp.where(p == 2, turn, jnp.where((p == 3) & (turn < 2), 1 + turn, from_chip))
            b = jnp.where(lead, c - 1, 2 * from_chip + jnp.where(odd == 0, k, 1 - k))
            b = jnp.where(b < 0, 0, b)

            @pl.when(step == 0)
            def _():
                for g in range(G):
                    kv_copy(b, g, k_send.at[0], sibling).wait_recv()

                    if relays:
                        @pl.when(((p == 1 + k) & (b == k)) | ((p == 3) & (b == 2 + k)))
                        def _():
                            kv_copy(b, g, k_relay, relay_target).start()

                    @pl.when(jnp.logical_not(lead) & (odd == 0))
                    def _():
                        kv_copy(b, g, k_fwd.at[b // 2], sibling).start()

            edge = (b == c - 1) | (b == 0)

            @pl.when(edge)
            def _():
                for g in range(G):
                    attend(g, r, b, "edge")

            @pl.when(jnp.logical_not(edge))
            def _():
                for g in range(G):
                    attend(g, r, b, "middle")

            return inner

        lax.fori_loop(0, c, one_block, 0)
        for g in range(G):
            o = acc_ref[g] / jnp.sum(l_ref[g], axis=-1, keepdims=True)
            for h in range(R):
                mixed[step, :, (g * R + h) * HD : (g * R + h + 1) * HD] = o[h].astype(jnp.bfloat16)

        inner_device = (z > 0) & (z < H - 1)
        ahead_to = jnp.where(step == H - 1, H, jnp.where(step < 2, 0, step))
        ahead_from = jnp.where(step <= 2, 0, step - 1)
        first = jnp.where(inner_device, ahead_from, step)
        last = jnp.where(inner_device, ahead_to, step + 1)
        lax.fori_loop(first, last, project, 0)
        return carry

    def project(step, carry):
        r = pick(table, z, step)
        has_a = ((r > z) & (z > 0)) | ((r < z) & (z < H - 1)) | ((r == z) & (z > 0))
        has_b = (r == z) & (z < H - 1)

        def piece(n, inner):
            @pl.when(step == 0)
            def _():
                w_copy(n).wait()

            tmp[...] = jnp.dot(mixed[step], w[n], preferred_element_type=jnp.float32)

            @pl.when(has_a)
            def _():
                part_wait(r, n)
                tmp[...] += part[r, n].astype(jnp.float32)

            @pl.when(has_b)
            def _():
                part_wait(H, n)
                tmp[...] += part[H, n].astype(jnp.float32)

            @pl.when(r == z)
            def _():
                out_ref[n] = tmp[...].astype(jnp.bfloat16)
                out_copy(n).start()

            @pl.when(r != z)
            def _():
                part[r, n] = tmp[...].astype(jnp.bfloat16)
                part_copy(r, n).start()

            return inner

        lax.fori_loop(0, NP, piece, 0)
        return carry

    lax.fori_loop(0, H, chunk, 0)

    for g in range(G):
        for q in range(chips):
            @pl.when(pushes(q))
            def _():
                kv_copy(c, g, k_send.at[q], 2 * q + k).wait_send()

            @pl.when(q < p)
            def _():
                kv_copy(2 * q + k, g, k_fwd.at[q], sibling).wait_send()

        @pl.when(k == 0)
        def _():
            kv_copy(c, g, k_send.at[p], sibling).wait_send()

        if relays:
            @pl.when((p == 1 + k) | (p == 3))
            def _():
                kv_copy(jnp.where(p == 3, 2 + k, k), g, k_relay, relay_target).wait_send()

    def drain(i, carry):
        @pl.when(i // NP != z)
        def _():
            part_copy(i // NP, i % NP).wait_send()

        return carry

    lax.fori_loop(0, H * NP, drain, 0)
    for n in range(NP):
        out_copy(n).wait()


def solution(mesh):
    C, H = mesh.shape["ctx"], mesh.shape["head"]

    def shards(queries, keys, values, gate_mask, w_out):
        T = queries.shape[0]
        G = keys.shape[1] // HD
        R = queries.shape[1] // keys.shape[1]
        K, D = w_out.shape
        rows = T // H
        NP = 8
        hbm = pl.BlockSpec(memory_space=pl.ANY)
        return pl.pallas_call(
            functools.partial(kernel, C, H, G, R, T, NP, D),
            out_shape=jax.ShapeDtypeStruct((rows, D), jnp.bfloat16),
            in_specs=[pl.BlockSpec(memory_space=pltpu.SMEM), hbm, hbm, hbm, hbm],
            out_specs=hbm,
            scratch_shapes=[
                pltpu.VMEM((T, G * R * HD), jnp.bfloat16),
                pltpu.VMEM((NP, rows, D // NP), jnp.bfloat16),
                pltpu.VMEM((C, G, 2, T, HD), jnp.bfloat16),
                pltpu.VMEM((NP, K, D // NP), jnp.bfloat16),
                pltpu.VMEM((H + 1, NP, rows, D // NP), jnp.bfloat16),
                pltpu.VMEM((G * R, rows, HD), jnp.float32),
                pltpu.VMEM((G, R, rows, HD), jnp.float32),
                pltpu.VMEM((G, R, rows, HD), jnp.float32),
                pltpu.VMEM((G, R, rows, HD), jnp.float32),
                pltpu.VMEM((H, rows, K), jnp.bfloat16),
                pltpu.VMEM((rows, D // NP), jnp.float32),
                pltpu.SemaphoreType.DMA,
                pltpu.SemaphoreType.DMA((2, G)),
                pltpu.SemaphoreType.DMA((NP,)),
                pltpu.SemaphoreType.DMA((NP,)),
                pltpu.SemaphoreType.DMA((C, G)),
                pltpu.SemaphoreType.DMA((C // 2, G)),
                pltpu.SemaphoreType.DMA((C // 2, G)),
                pltpu.SemaphoreType.DMA((G,)),
                pltpu.SemaphoreType.DMA((H, NP)),
                pltpu.SemaphoreType.DMA((H + 1, NP)),
            ],
            compiler_params=pltpu.CompilerParams(
                collective_id=0, has_side_effects=True, vmem_limit_bytes=60 * 2**20
            ),
        )(gate_mask, queries, keys, values, w_out)

    in_specs = (P("ctx", "head"), P("ctx", "head"), P("ctx", "head"), P("head"), P("head", None))
    out_specs = P(("ctx", "head"), None)
    return jax.shard_map(shards, mesh=mesh, in_specs=in_specs, out_specs=out_specs, check_vma=False)
```
